32 devices in a mesh: grp: 2 (over x), tm: 16 (over z, y, core).
Axes of the slice: x: 2, y: 2, z: 4, core: 2. Of those that a mesh axis runs over, the one named last changes fastest.
Arguments:
- states: float32 [32, 84, 12, 128], P(('grp', 'tm')), parts along dimension 0, may hold values from -6 to 6
- slab_steps: int32 [32], P(('grp', 'tm')), parts along dimension 0, may hold values from 0 to 999
- offset: int32 [2], P('grp'), parts along dimension 0, may hold values from 0 to 999
- log_sigma: float32 [1000], replicated, may hold values from -2 to 2
- step_size: float32 [1000], replicated, may hold values from -0.12 to -0.03
- w_in: bfloat16 [9, 256, 84], replicated, may hold values from -0.21875 to 0.21875
- w_mid: bfloat16 [9, 256, 256], replicated, may hold values from -0.125 to 0.125
- w_out: bfloat16 [9, 84, 256], replicated, may hold values from -0.125 to 0.125
- embed: float32 [256], replicated, may hold values from -5 to 5
Outputs:
- new_states: float32 [32, 84, 12, 128], P(('grp', 'tm')), parts along dimension 0
The draws below stay inside these ranges and needn't reach their ends.
There are 2 independent parts, one for each index of `grp`. The reference program is written for one: setup_inputs(seed, part) draws one part's arguments, and reference() takes and returns one part's arrays. A program takes and returns all parts, laid end to end along the dimension named above; an argument that names none is the same for every part. Nothing has to cross between parts.
All inputs are finite; a program needn't handle non-finite values.
Results may differ from the reference program's by a relative error of at most 0.0011.
Values sent between devices are 32-bit elements; how exact they have to be, the bound alone decides.
No kernel may reach another device: no remote copies, remote signals or barrier semaphores. Data moves between devices by JAX's collectives and lax.ppermute only.
A program may use at most 64 MiB of HBM per device.

```python
import jax
import jax.numpy as jnp
from jax import lax

F = 84
CH = 256
H = 12
W = 128
TABLE = 1000
SWEEPS = 2
SLABS = 16


def plant(entries, key, least, largest):
    index_at = [jax.random.randint(jax.random.fold_in(key, axis), (), 0, length) for axis, length in enumerate(entries.shape)]
    longest = entries.shape.index(max(entries.shape))
    neighbour = index_at[:longest] + [(index_at[longest] + 1) % entries.shape[longest]] + index_at[longest + 1:]
    return entries.at[tuple(index_at)].set(least).at[tuple(neighbour)].set(largest)


def steps_of(key, extent, split, low, largest):
    def one(dim, shards_of):
        steps = jax.random.uniform(jax.random.fold_in(jax.random.fold_in(key, 6), dim), (shards_of,), jnp.float32, low / len(split), largest / len(split))
        return jnp.repeat(jnp.exp(steps), extent[dim] // shards_of).reshape((-1,) + (1,) * (len(extent) - dim - 1))

    level = one(*split[0])
    for cut in split[1:]:
        level = level * one(*cut)
    return level


def noise(key, shape, scale, bound, pieces=(), held_as=jnp.bfloat16):
    factor_of = steps_of(key, shape, pieces, -0.22, 0.18) if pieces else 1.0
    values = jax.random.normal(key, shape, jnp.float32) * scale * factor_of
    return jnp.minimum(jnp.maximum(values, -bound), bound).astype(held_as)


def setup_inputs(seed: int = 0, part: int = 0) -> dict:
    keys = jax.random.split(jax.random.key(seed), 10)
    own_keys = jax.random.split(jax.random.fold_in(keys[9], part), 10)
    return {
        "states": noise(own_keys[0], (SLABS, F, H, W), 1.0, 6.0, ((0, 16),), jnp.float32),
        "slab_steps": plant(jax.random.randint(own_keys[1], (SLABS,), 0, TABLE), jax.random.fold_in(own_keys[1], 1), 0, TABLE - 1).astype(jnp.int32),
        "offset": jax.random.randint(own_keys[2], (1,), 0, TABLE).astype(jnp.int32),
        "log_sigma": jnp.clip(jax.random.uniform(keys[3], (TABLE,), jnp.float32, -2.0, 2.0), -2.0, 2.0),
        "step_size": jnp.clip(jax.random.uniform(keys[4], (TABLE,), jnp.float32, -0.12, -0.03), -0.12, -0.03),
        "w_in": noise(keys[5], (9, CH, F), (9 * F) ** -0.5, 0.21875),
        "w_mid": noise(keys[6], (9, CH, CH), (9 * CH) ** -0.5, 0.125),
        "w_out": noise(keys[7], (9, F, CH), (9 * CH) ** -0.5, 0.125),
        "embed": noise(keys[8], (CH,), 1.0, 5.0, (), jnp.float32),
    }


def convolve(field, weights):
    channels = field.shape[0]
    padded = jnp.pad(field, ((0, 0), (1, 1), (1, 1)))
    total = jnp.zeros((weights.shape[1], H * W), jnp.float32)
    for kernel_tap in range(9):
        row_shift = kernel_tap // 3
        col_shift = kernel_tap % 3
        window = padded[:, row_shift:row_shift + H, col_shift:col_shift + W].reshape(channels, H * W)
        total = total + jnp.dot(weights[kernel_tap], window, preferred_element_type=jnp.float32)
    return total


def drift_field(field, log_noise, w_in, w_mid, w_out, embed):
    first = convolve(field.astype(jnp.bfloat16), w_in) + log_noise * embed[:, None]
    first = jax.nn.silu(first).astype(jnp.bfloat16).reshape(CH, H, W)
    second = jax.nn.silu(convolve(first, w_mid)).astype(jnp.bfloat16).reshape(CH, H, W)
    return convolve(second, w_out).reshape(F, H, W)


def reference(states, slab_steps, offset, log_sigma, step_size, w_in, w_mid, w_out, embed):
    table_row = ((slab_steps + offset[0]) % TABLE).astype(jnp.int32)
    log_noise = log_sigma[table_row]
    step_len = step_size[table_row]
    field = states
    through = states
    for sweep_index in range(SWEEPS):
        drifts = lax.map(lambda operands: drift_field(operands[0], operands[1], w_in, w_mid, w_out, embed), (field, log_noise))
        increments = step_len[:, None, None, None] * drifts
        increments = increments.at[0].add(field[0])
        through = jnp.cumsum(increments, axis=0)
        if sweep_index + 1 < SWEEPS:
            field = jnp.concatenate([field[:1], through[:-1]], axis=0)
    return through
```

```python
import jax
import jax.numpy as jnp
from jax import lax
from jax.experimental import pallas as pl
from jax.experimental.pallas import tpu as pltpu
from jax.sharding import PartitionSpec as P

SWEEPS = 2


def up(v, m):
    return -(-v // m) * m


def sweep_kernel(dims, x_ref, step_ref, off_ref, owner_ref, ls_ref, h_ref, emb_ref, w1_ref, w2_ref, w3_ref,
                 o_ref, w1s, w3s, xs, u1, u2):
    fields, hidden, rows, cols, table, per = dims
    kin = up(3 * fields, 16)
    mout = up(fields, 16)
    wide = per * cols
    lane = lax.broadcasted_iota(jnp.int32, (1, cols), 1)
    first_col = lane == 0
    last_col = lane == cols - 1

    def right(v):
        return jnp.where(first_col, 0.0, pltpu.roll(v, 1, 1))

    def left(v):
        return jnp.where(last_col, 0.0, pltpu.roll(v, cols - 1, 1))

    total = step_ref[0] + off_ref[0]
    row = jnp.where(total >= table, total - table, total)
    log_noise = ls_ref[row]
    step_len = h_ref[row]
    is_first = owner_ref[0] == 0

    for a in range(3):
        parts = [w1_ref[3 * a + b].astype(jnp.float32) for b in range(3)]
        pad = kin - 3 * fields
        if pad:
            parts.append(jnp.zeros((pad, hidden), jnp.float32))
        w1s[a] = jnp.concatenate(parts, axis=0).astype(jnp.bfloat16)
        for b in range(3):
            w3s[a, b * mout:b * mout + fields, :] = w3_ref[3 * a + b]
            if mout > fields:
                w3s[a, b * mout + fields:(b + 1) * mout, :] = jnp.zeros((mout - fields, hidden), jnp.bfloat16)
    bias = []
    for t in range(hidden // cols):
        e = emb_ref[t:t + 1, :] * log_noise
        bias.append(jnp.broadcast_to(e, (cols, cols)).T)
    bias = jnp.concatenate(bias, axis=0)
    bias = jnp.concatenate([bias] * per, axis=1)

    zx = jnp.zeros((kin, cols), jnp.bfloat16)
    zu = jnp.zeros((hidden, cols), jnp.bfloat16)
    for edge in (0, (rows + 1) * cols):
        xs[:, edge:edge + cols] = zx
        u2[:, edge:edge + cols] = zu
        for b in range(3):
            u1[b, :, edge:edge + cols] = zu

    def load_row(r):
        v = x_ref[pl.ds(r, fields, stride=rows), :]
        parts = [right(v), v, left(v)]
        if kin > 3 * fields:
            parts.append(jnp.zeros((kin - 3 * fields, cols), jnp.float32))
        xs[:, (r + 1) * cols:(r + 2) * cols] = jnp.concatenate(parts, axis=0).astype(jnp.bfloat16)

    def silu(t):
        return t / (1.0 + jnp.exp(-t))

    def conv1(n):
        acc = None
        for a in range(3):
            lo = (n * per + a) * cols
            d = lax.dot_general(w1s[a], xs[:, lo:lo + wide], (((0,), (0,)), ((), ())),
                                preferred_element_type=jnp.float32)
            acc = d if acc is None else acc + d
        u = silu(acc + bias)
        for i in range(per):
            lo = (n * per + i + 1) * cols
            v = u[:, i * cols:(i + 1) * cols]
            u1[0, :, lo:lo + cols] = right(v).astype(jnp.bfloat16)
            u1[1, :, lo:lo + cols] = v.astype(jnp.bfloat16)
            u1[2, :, lo:lo + cols] = left(v).astype(jnp.bfloat16)

    def conv2(n):
        acc = None
        for a in range(3):
            lo = (n * per + a) * cols
            for b in range(3):
                d = jnp.dot(w2_ref[3 * a + b], u1[b, :, lo:lo + wide], preferred_element_type=jnp.float32)
                acc = d if acc is None else acc + d
        lo = (n * per + 1) * cols
        u2[:, lo:lo + wide] = silu(acc).astype(jnp.bfloat16)

    def conv3(n):
        acc = None
        for a in range(3):
            lo = (n * per + a) * cols
            d = jnp.dot(w3s[a], u2[:, lo:lo + wide], preferred_element_type=jnp.float32)
            acc = d if acc is None else acc + d
        for i in range(per):
            y = acc[:, i * cols:(i + 1) * cols]
            out = right(y[:fields]) + y[mout:mout + fields] + left(y[2 * mout:2 * mout + fields])
            r = n * per + i
            own = x_ref[pl.ds(r, fields, stride=rows), :]
            o_ref[pl.ds(r, fields, stride=rows), :] = step_len * out + jnp.where(is_first, own, 0.0)

    blocks = rows // per
    for r in range(rows):
        load_row(r)
    for n in range(blocks + 2):
        if n < blocks:
            conv1(n)
        if 1 <= n < blocks + 1:
            conv2(n - 1)
        if n >= 2:
            conv3(n - 2)


def sweep(x, slab_steps, offset, owner, log_sigma, step_size, embed, w1t, w2, w3, rows, per=2):
    cols = x.shape[1]
    fields = x.shape[0] // rows
    hidden = w2.shape[1]
    table = log_sigma.shape[0]
    kin = up(3 * fields, 16)
    mout = up(fields, 16)
    dims = (fields, hidden, rows, cols, table, per)
    smem = pl.BlockSpec(memory_space=pltpu.SMEM)
    vmem = pl.BlockSpec(memory_space=pltpu.VMEM)
    flops = 2 * rows * cols * 9 * hidden * (2 * fields + hidden)
    return pl.pallas_call(
        lambda *refs: sweep_kernel(dims, *refs),
        out_shape=jax.ShapeDtypeStruct(x.shape, jnp.float32),
        in_specs=[vmem, smem, smem, smem, smem, smem, vmem, vmem, vmem, vmem],
        out_specs=vmem,
        scratch_shapes=[
            pltpu.VMEM((3, kin, hidden), jnp.bfloat16),
            pltpu.VMEM((3, 3 * mout, hidden), jnp.bfloat16),
            pltpu.VMEM((kin, (rows + 2) * cols), jnp.bfloat16),
            pltpu.VMEM((3, hidden, (rows + 2) * cols), jnp.bfloat16),
            pltpu.VMEM((hidden, (rows + 2) * cols), jnp.bfloat16),
        ],
        compiler_params=pltpu.CompilerParams(vmem_limit_bytes=48 << 20),
        cost_estimate=pl.CostEstimate(flops=flops, transcendentals=2 * hidden * rows * cols, bytes_accessed=4 << 20),
        name="sweep",
    )(x, slab_steps, offset, owner, log_sigma, step_size, embed.reshape(-1, cols), w1t, w2, w3)


def partner(axis, step):
    return [(j, j ^ step) for j in range(lax.axis_size(axis))]


def swap(value, step):
    return lax.ppermute(value, "tm", partner("tm", step))


def earlier_sum(increment, owner):
    owners = lax.axis_size("tm")
    length = increment.shape[0]
    half = length // 2
    quarter = up(half // 2, 8)
    core = owner & 1
    side = (owner >> 1) & 1
    mate = swap(increment, 1)
    pair = increment + mate
    mine = core * half + side * (half - quarter)
    theirs = core * half + (1 - side) * (half - quarter)
    own = lax.dynamic_slice_in_dim(pair, mine, quarter, 0)
    got = swap(lax.dynamic_slice_in_dim(pair, theirs, quarter, 0), 2)
    total = own + got
    before = jnp.zeros_like(total)
    step = 4
    while step < owners:
        far = swap(total, step)
        before = before + jnp.where((owner & step) != 0, far, 0.0)
        total = total + far
        step *= 2
    back = swap(before + jnp.where(side == 0, own, 0.0), 2)
    here = before + jnp.where(side == 1, got, 0.0)
    low = jnp.where(side == 0, here, back)
    high = jnp.where(side == 0, back, here)
    part = jnp.concatenate([low[: half - quarter], high], axis=0)
    rest = swap(part, 1)
    full = jnp.where(core == 0, jnp.concatenate([part, rest], axis=0), jnp.concatenate([rest, part], axis=0))
    return full + jnp.where(core == 1, mate, 0.0)


def shards(states, slab_steps, offset, log_sigma, step_size, w_in, w_mid, w_out, embed):
    owner = lax.axis_index("tm")
    _, fields, rows, cols = states.shape
    field = states.reshape(fields * rows, cols)
    where = owner.reshape(1).astype(jnp.int32)
    w1t = w_in.transpose(0, 2, 1)
    for sweep_index in range(SWEEPS):
        increment = sweep(field, slab_steps, offset, where, log_sigma, step_size, embed, w1t, w_mid, w_out, rows)
        before = earlier_sum(increment, owner)
        if sweep_index + 1 < SWEEPS:
            field = jnp.where(owner == 0, field, before)
    return (before + increment).reshape(states.shape)


def solution(mesh):
    in_specs = (
        P(("grp", "tm"), None, None, None),
        P(("grp", "tm")),
        P("grp"),
        P(),
        P(),
        P(),
        P(),
        P(),
        P(),
    )
    out_specs = P(("grp", "tm"), None, None, None)
    return jax.shard_map(shards, mesh=mesh, in_specs=in_specs, out_specs=out_specs, check_vma=False)
```

```python
import jax
import jax.numpy as jnp
from jax import lax
from jax.experimental import pallas as pl
from jax.experimental.pallas import tpu as pltpu
from jax.sharding import PartitionSpec as P


SWEEPS = 2
BF16 = jnp.bfloat16
F32 = jnp.float32


def up(v, m):
    return -(-v // m) * m


class Sizes:
    def __init__(self, fields, hidden, rows, cols, table):
        self.fields, self.hidden, self.rows, self.cols, self.table = fields, hidden, rows, cols, table
        self.per = 2 if rows % 2 == 0 else 1
        self.blocks = rows // self.per
        self.wide = self.per * cols
        self.kin = up(3 * fields, 16)
        self.mout = up(fields, 16)
        self.cut = (self.blocks + 1) // 2
        self.chunks = ((0, self.cut * self.per), (self.cut * self.per, rows))
        self.long = (rows + 2) * cols


class Body:
    def __init__(self, z, w1s, w2, w3s, bias, par, xs, u1, u2):
        self.z, self.w1s, self.w2, self.w3s, self.bias, self.par = z, w1s, w2, w3s, bias, par
        self.xs, self.u1, self.u2 = xs, u1, u2
        lane = lax.broadcasted_iota(jnp.int32, (1, z.cols), 1)
        self.first_col = lane == 0
        self.last_col = lane == z.cols - 1

    def right(self, v):
        return jnp.where(self.first_col, 0.0, pltpu.roll(v, 1, 1))

    def left(self, v):
        return jnp.where(self.last_col, 0.0, pltpu.roll(v, self.z.cols - 1, 1))

    def clear_edges(self):
        z = self.z
        zx = jnp.zeros((z.kin, z.cols), BF16)
        zu = jnp.zeros((z.hidden, z.cols), BF16)
        for edge in (0, (z.rows + 1) * z.cols):
            self.xs[:, edge:edge + z.cols] = zx
            self.u2[:, edge:edge + z.cols] = zu
            for b in range(3):
                self.u1[b, :, edge:edge + z.cols] = zu

    def load_row(self, r, v):
        z = self.z
        parts = [self.right(v), v, self.left(v)]
        if z.kin > 3 * z.fields:
            parts.append(jnp.zeros((z.kin - 3 * z.fields, z.cols), F32))
        self.xs[:, (r + 1) * z.cols:(r + 2) * z.cols] = jnp.concatenate(parts, axis=0).astype(BF16)

    def silu(self, t):
        return t / (1.0 + jnp.exp(-t))

    def conv1(self, n):
        z = self.z
        acc = None
        for a in range(3):
            lo = (n * z.per + a) * z.cols
            d = lax.dot_general(self.w1s[a], self.xs[:, lo:lo + z.wide], (((0,), (0,)), ((), ())),
                                preferred_element_type=F32)
            acc = d if acc is None else acc + d
        for i in range(z.per):
            lo = (n * z.per + i + 1) * z.cols
            v = self.silu(acc[:, i * z.cols:(i + 1) * z.cols] + self.bias[...])
            self.u1[0, :, lo:lo + z.cols] = self.right(v).astype(BF16)
            self.u1[1, :, lo:lo + z.cols] = v.astype(BF16)
            self.u1[2, :, lo:lo + z.cols] = self.left(v).astype(BF16)

    def conv2(self, n):
        z = self.z
        acc = None
        for a in range(3):
            lo = (n * z.per + a) * z.cols
            for b in range(3):
                d = jnp.dot(self.w2[3 * a + b], self.u1[b, :, lo:lo + z.wide], preferred_element_type=F32)
                acc = d if acc is None else acc + d
        lo = (n * z.per + 1) * z.cols
        self.u2[:, lo:lo + z.wide] = self.silu(acc).astype(BF16)

    def conv3(self, n, emit):
        z = self.z
        acc = None
        for a in range(3):
            lo = (n * z.per + a) * z.cols
            d = jnp.dot(self.w3s[a], self.u2[:, lo:lo + z.wide], preferred_element_type=F32)
            acc = d if acc is None else acc + d
        for i in range(z.per):
            y = acc[:, i * z.cols:(i + 1) * z.cols]
            out = self.right(y[:z.fields]) + y[z.mout:z.mout + z.fields] + self.left(y[2 * z.mout:2 * z.mout + z.fields])
            emit(n * z.per + i, out * self.par[0:1, :])

    def run(self, begin, end, emit, before2=None, before3=None):
        for n in range(self.z.blocks + 2):
            if begin[0] <= n < end[0]:
                self.conv1(n)
            if begin[1] <= n - 1 < end[1]:
                if before2 is not None:
                    before2()
                    before2 = None
                self.conv2(n - 1)
            if begin[2] <= n - 2 < end[2]:
                if before3 is not None:
                    before3()
                    before3 = None
                self.conv3(n - 2, emit)


def own_rows(z, x_ref, r):
    return x_ref[pl.ds(r, z.fields, stride=z.rows), :]


def put_row(z, chunk, out_ref, r, v):
    lo, hi = z.chunks[chunk]
    out_ref[pl.ds(r - lo, z.fields, stride=hi - lo), :] = v


def get_row(z, chunk, in_ref, r):
    lo, hi = z.chunks[chunk]
    return in_ref[pl.ds(r - lo, z.fields, stride=hi - lo), :]


def clip(z, cut):
    return min(cut + 2, z.blocks), min(cut + 1, z.blocks), cut


def open_kernel(z, x_hbm, step_ref, off_ref, owner_ref, place0, place1, place2, place3, ls_hbm, h_hbm, emb_hbm, w1_hbm, w2_hbm, w3_hbm,
                inc_ref, x_ref, w1s, w2v, w3s, bias, par, xs, u1, u2,
                ls_ref, h_ref, emb_ref, w1_ref, w3_ref, sems):
    copies = [pltpu.make_async_copy(src, dst, sems.at[k]) for k, (src, dst) in enumerate([
        (ls_hbm, ls_ref), (h_hbm, h_ref), (emb_hbm, emb_ref), (x_hbm, x_ref), (w1_hbm, w1_ref),
        (w2_hbm, w2v), (w3_hbm, w3_ref)])]
    for copy in copies:
        copy.start()
    body = Body(z, w1s, w2v, w3s, bias, par, xs, u1, u2)
    body.clear_edges()
    for copy in copies[:3]:
        copy.wait()
    total = step_ref[0] + off_ref[0]
    row = jnp.where(total >= z.table, total - z.table, total)
    log_noise = ls_ref[row]
    par[0:1, :] = jnp.full((1, z.cols), h_ref[row], F32)
    par[1:2, :] = jnp.where(owner_ref[0] == 0, jnp.ones((1, z.cols), F32), jnp.zeros((1, z.cols), F32))
    for t in range(z.hidden // z.cols):
        e = emb_ref[t:t + 1, :] * log_noise
        bias[t * z.cols:(t + 1) * z.cols, :] = jnp.broadcast_to(e, (z.cols, z.cols)).T
    copies[3].wait()
    for r in range(z.rows):
        body.load_row(r, own_rows(z, x_ref, r))
    copies[4].wait()
    for a in range(3):
        parts = [w1_ref[3 * a + b].astype(F32) for b in range(3)]
        if z.kin > 3 * z.fields:
            parts.append(jnp.zeros((z.kin - 3 * z.fields, z.hidden), F32))
        w1s[a] = jnp.concatenate(parts, axis=0).astype(BF16)

    def before3():
        copies[6].wait()
        for a in range(3):
            for b in range(3):
                w3s[a, b * z.mout:b * z.mout + z.fields, :] = w3_ref[3 * a + b]
                if z.mout > z.fields:
                    w3s[a, b * z.mout + z.fields:(b + 1) * z.mout, :] = jnp.zeros((z.mout - z.fields, z.hidden), BF16)

    is_first = par[1:2, :] > 0.0

    def emit(r, v):
        put_row(z, 0, inc_ref, r, v + jnp.where(is_first, own_rows(z, x_ref, r), 0.0))

    body.run((0, 0, 0), clip(z, z.cut), emit, copies[5].wait, before3)


def close_kernel(z, x_ref, w1s, w2, w3s, bias, par, xs_in, u1_in, u2_in, inc_ref, xs, u1, u2):
    body = Body(z, w1s, w2, w3s, bias, par, xs, u1, u2)
    is_first = par[1:2, :] > 0.0

    def emit(r, v):
        put_row(z, 1, inc_ref, r, v + jnp.where(is_first, own_rows(z, x_ref, r), 0.0))

    body.run(clip(z, z.cut), (z.blocks,) * 3, emit)


def later_kernel(z, x_ref, f0_ref, f1_ref, w1s, w2_hbm, w3s, bias, par, inc_ref, w2, xs, u1, u2, sem):
    copy = pltpu.make_async_copy(w2_hbm, w2, sem)
    copy.start()
    body = Body(z, w1s, w2, w3s, bias, par, xs, u1, u2)
    body.clear_edges()
    is_first = par[1:2, :] > 0.0
    for chunk, ref in enumerate((f0_ref, f1_ref)):
        for r in range(*z.chunks[chunk]):
            body.load_row(r, jnp.where(is_first, own_rows(z, x_ref, r), get_row(z, chunk, ref, r)))

    def emit(r, v):
        put_row(z, 0, inc_ref, r, v + jnp.where(is_first, own_rows(z, x_ref, r), 0.0))

    body.run((0, 0, 0), clip(z, z.cut), emit, copy.wait)


def merge_kernel(z, a_ref, b_ref, o_ref):
    for chunk, ref in enumerate((a_ref, b_ref)):
        for r in range(*z.chunks[chunk]):
            o_ref[pl.ds(r, z.fields, stride=z.rows), :] = get_row(z, chunk, ref, r)


VMEM = pl.BlockSpec(memory_space=pltpu.VMEM)
SMEM = pl.BlockSpec(memory_space=pltpu.SMEM)
HBM = pl.BlockSpec(memory_space=pltpu.HBM)


def shape(*dims, dtype=F32):
    return jax.ShapeDtypeStruct(dims, dtype)


def params():
    return pltpu.CompilerParams(vmem_limit_bytes=20 << 20)


def cost(z, share):
    flops = int(share * 2 * z.rows * z.cols * 9 * z.hidden * (2 * z.fields + z.hidden))
    return pl.CostEstimate(flops=flops, transcendentals=int(share * 2 * z.hidden * z.rows * z.cols), bytes_accessed=1 << 20)


class Program:
    def __init__(self, z):
        self.z = z
        self.state = [shape(z.kin, z.long, dtype=BF16), shape(3, z.hidden, z.long, dtype=BF16), shape(z.hidden, z.long, dtype=BF16)]

    def chunk_shape(self, chunk):
        lo, hi = self.z.chunks[chunk]
        return shape(self.z.fields * (hi - lo), self.z.cols)

    def open(self, x, slab_steps, offset, owner, places, log_sigma, step_size, embed, w1t, w2, w3):
        z = self.z
        outs = [self.chunk_shape(0), shape(*x.shape), shape(3, z.kin, z.hidden, dtype=BF16), shape(*w2.shape, dtype=BF16),
                shape(3, 3 * z.mout, z.hidden, dtype=BF16), shape(z.hidden, z.cols), shape(8, z.cols)] + self.state
        far = [pltpu.with_memory_space_constraint(v, pltpu.HBM) for v in (log_sigma, step_size, embed, w1t, w2, w3)]
        res = pl.pallas_call(
            lambda *refs: open_kernel(z, *refs), out_shape=outs,
            in_specs=[HBM, SMEM, SMEM, SMEM] + [SMEM] * 4 + [HBM] * 6, out_specs=[VMEM] * len(outs),
            scratch_shapes=[pltpu.SMEM((z.table,), F32), pltpu.SMEM((z.table,), F32), pltpu.VMEM(embed.shape, F32),
                            pltpu.VMEM(w1t.shape, BF16), pltpu.VMEM(w3.shape, BF16), pltpu.SemaphoreType.DMA((7,))],
            compiler_params=params(), cost_estimate=cost(z, 0.7), name="open",
        )(pltpu.with_memory_space_constraint(x, pltpu.HBM), slab_steps, offset, owner, *[v.reshape(1) for v in places], *far)
        self.w2 = res[3]
        self.fixed = list(res[2:7])
        self.x = res[1]
        return res[0], list(res[7:])

    def close(self, state):
        z = self.z
        ins = [self.x, *self.fixed, *state]
        outs = [self.chunk_shape(1)] + self.state
        res = pl.pallas_call(
            lambda *refs: close_kernel(z, *refs), out_shape=outs, in_specs=[VMEM] * len(ins), out_specs=[VMEM] * len(outs),
            input_output_aliases={len(ins) - 3 + k: 1 + k for k in range(3)},
            compiler_params=params(), cost_estimate=cost(z, 0.3), name="close",
        )(*ins)
        return res[0]

    def later(self, x, w2, sum0, sum1):
        z = self.z
        self.x = x
        self.fixed[1] = pltpu.with_memory_space_constraint(w2, pltpu.HBM)
        ins = [x, sum0, sum1, *self.fixed]
        outs = [self.chunk_shape(0), shape(*w2.shape, dtype=BF16)] + self.state
        specs = [VMEM] * 4 + [HBM] + [VMEM] * 3
        res = pl.pallas_call(
            lambda *refs: later_kernel(z, *refs), out_shape=outs, in_specs=specs, out_specs=[VMEM] * len(outs),
            scratch_shapes=[pltpu.SemaphoreType.DMA],
            compiler_params=params(), cost_estimate=cost(z, 0.7), name="later",
        )(*ins)
        self.fixed[1] = res[1]
        return res[0], list(res[2:])

    def merge(self, a, b):
        z = self.z
        return pl.pallas_call(
            lambda *refs: merge_kernel(z, *refs), out_shape=shape(z.fields * z.rows, z.cols),
            in_specs=[VMEM, VMEM], out_specs=VMEM, compiler_params=params(), name="merge",
        )(a, b)


def swap(value, step):
    return lax.ppermute(value, "tm", [(j, j ^ step) for j in range(lax.axis_size("tm"))])


def places_of(owner, length):
    half = up(length // 2, 8)
    quarter = up(half // 2, 8)
    base = (owner & 1) * (length - half)
    side = (owner >> 1) & 1
    return base + side * (half - quarter), base + (1 - side) * (half - quarter)


def earlier_sum(increment, owner, places):
    owners = lax.axis_size("tm")
    length = increment.shape[0]
    half = up(length // 2, 8)
    quarter = up(half // 2, 8)
    core = owner & 1
    side = (owner >> 1) & 1
    mate = swap(increment, 1)
    pair = increment + mate
    own = lax.dynamic_slice(pair, (places[0], 0), (quarter, pair.shape[1]), allow_negative_indices=False)
    theirs = lax.dynamic_slice(pair, (places[1], 0), (quarter, pair.shape[1]), allow_negative_indices=False)
    got = swap(theirs, 2)
    total = own + got
    before = jnp.zeros_like(total)
    for k in range(2, owners.bit_length() - 1):
        far = swap(total, 1 << k)
        before = before + jnp.where((owner & (1 << k)) != 0, far, 0.0)
        total = total + far
    back = swap(before + jnp.where(side == 0, own, 0.0), 2)
    here = before + jnp.where(side == 1, got, 0.0)
    low = jnp.where(side == 0, here, back)
    high = jnp.where(side == 0, back, here)
    part = jnp.concatenate([low[: half - quarter], high], axis=0)
    rest = swap(part, 1)
    low = jnp.where(core == 0, part, rest)
    high = jnp.where(core == 0, rest, part)
    full = jnp.concatenate([low[: length - half], high], axis=0)
    return full + jnp.where(core == 1, mate, 0.0)


def shards(states, slab_steps, offset, log_sigma, step_size, w_in, w_mid, w_out, embed):
    owner = lax.axis_index("tm")
    _, fields, rows, cols = states.shape
    z = Sizes(fields, w_in.shape[1], rows, cols, log_sigma.shape[0])
    program = Program(z)
    where = owner.reshape(1).astype(jnp.int32)
    x = states.reshape(fields * rows, cols)
    places = [places_of(owner, fields * (hi - lo)) for lo, hi in z.chunks]
    for sweep_index in range(SWEEPS):
        if sweep_index == 0:
            inc0, state = program.open(x, slab_steps, offset, where, (*places[0], *places[1]), log_sigma, step_size, embed.reshape(-1, cols),
                                       w_in.transpose(0, 2, 1), w_mid, w_out)
        else:
            inc0, state = program.later(x, w_mid, sum0, sum1)
        inc1 = program.close(state)
        sum0 = earlier_sum(inc0, owner, places[0])
        sum1 = earlier_sum(inc1, owner, places[1])
    return program.merge(sum0 + inc0, sum1 + inc1).reshape(states.shape)


def solution(mesh):
    in_specs = (
        P(("grp", "tm"), None, None, None),
        P(("grp", "tm")),
        P("grp"),
        P(),
        P(),
        P(),
        P(),
        P(),
        P(),
    )
    out_specs = P(("grp", "tm"), None, None, None)
    return jax.shard_map(shards, mesh=mesh, in_specs=in_specs, out_specs=out_specs, check_vma=False)
```

```python
import jax
import jax.numpy as jnp
from jax import lax
from jax.experimental import pallas as pl
from jax.experimental.pallas import tpu as pltpu
from jax.sharding import PartitionSpec as P


SWEEPS = 2
BF16 = jnp.bfloat16
F32 = jnp.float32


def up(v, m):
    return -(-v // m) * m


class Sizes:
    def __init__(self, fields, hidden, rows, cols, table):
        self.fields, self.hidden, self.rows, self.cols, self.table = fields, hidden, rows, cols, table
        self.per = 2 if rows % 2 == 0 else 1
        self.blocks = rows // self.per
        self.wide = self.per * cols
        self.kin = up(3 * fields, 16)
        self.mout = up(fields, 16)
        self.cut = (self.blocks + 1) // 2
        self.chunks = ((0, self.cut * self.per), (self.cut * self.per, rows))
        self.long = (rows + 2) * cols


class Body:
    def __init__(self, z, w1s, w2, w3s, bias, par, xs, u1, u2):
        self.z, self.w1s, self.w2, self.w3s, self.bias, self.par = z, w1s, w2, w3s, bias, par
        self.xs, self.u1, self.u2 = xs, u1, u2
        lane = lax.broadcasted_iota(jnp.int32, (1, z.cols), 1)
        self.first_col = lane == 0
        self.last_col = lane == z.cols - 1

    def right(self, v):
        return jnp.where(self.first_col, 0.0, pltpu.roll(v, 1, 1))

    def left(self, v):
        return jnp.where(self.last_col, 0.0, pltpu.roll(v, self.z.cols - 1, 1))

    def clear_edges(self):
        z = self.z
        zx = jnp.zeros((z.kin, z.cols), BF16)
        zu = jnp.zeros((z.hidden, z.cols), BF16)
        for edge in (0, (z.rows + 1) * z.cols):
            self.xs[:, edge:edge + z.cols] = zx
            self.u2[:, edge:edge + z.cols] = zu
            for b in range(3):
                self.u1[b, :, edge:edge + z.cols] = zu

    def load_row(self, r, v):
        z = self.z
        parts = [self.right(v), v, self.left(v)]
        if z.kin > 3 * z.fields:
            parts.append(jnp.zeros((z.kin - 3 * z.fields, z.cols), F32))
        self.xs[:, (r + 1) * z.cols:(r + 2) * z.cols] = jnp.concatenate(parts, axis=0).astype(BF16)

    def silu(self, t):
        return t / (1.0 + jnp.exp(-t))

    def conv1(self, n):
        z = self.z
        acc = None
        for a in range(3):
            lo = (n * z.per + a) * z.cols
            d = lax.dot_general(self.w1s[a], self.xs[:, lo:lo + z.wide], (((0,), (0,)), ((), ())),
                                preferred_element_type=F32)
            acc = d if acc is None else acc + d
        for i in range(z.per):
            lo = (n * z.per + i + 1) * z.cols
            v = self.silu(acc[:, i * z.cols:(i + 1) * z.cols] + self.bias[...])
            self.u1[0, :, lo:lo + z.cols] = self.right(v).astype(BF16)
            self.u1[1, :, lo:lo + z.cols] = v.astype(BF16)
            self.u1[2, :, lo:lo + z.cols] = self.left(v).astype(BF16)

    def conv2(self, n):
        z = self.z
        acc = None
        for a in range(3):
            lo = (n * z.per + a) * z.cols
            for b in range(3):
                d = jnp.dot(self.w2[3 * a + b], self.u1[b, :, lo:lo + z.wide], preferred_element_type=F32)
                acc = d if acc is None else acc + d
        lo = (n * z.per + 1) * z.cols
        self.u2[:, lo:lo + z.wide] = self.silu(acc).astype(BF16)

    def conv3(self, n, emit):
        z = self.z
        acc = None
        for a in range(3):
            lo = (n * z.per + a) * z.cols
            d = jnp.dot(self.w3s[a], self.u2[:, lo:lo + z.wide], preferred_element_type=F32)
            acc = d if acc is None else acc + d
        for i in range(z.per):
            y = acc[:, i * z.cols:(i + 1) * z.cols]
            out = self.right(y[:z.fields]) + y[z.mout:z.mout + z.fields] + self.left(y[2 * z.mout:2 * z.mout + z.fields])
            emit(n * z.per + i, out * self.par[0:1, :])

    def run(self, begin, end, emit, before2=None, before3=None):
        for n in range(self.z.blocks + 2):
            if begin[0] <= n < end[0]:
                self.conv1(n)
            if begin[1] <= n - 1 < end[1]:
                if before2 is not None:
                    before2()
                    before2 = None
                self.conv2(n - 1)
            if begin[2] <= n - 2 < end[2]:
                if before3 is not None:
                    before3()
                    before3 = None
                self.conv3(n - 2, emit)


def own_rows(z, x_ref, r):
    return x_ref[pl.ds(r, z.fields, stride=z.rows), :]


def put_row(z, chunk, out_ref, r, v):
    lo, hi = z.chunks[chunk]
    out_ref[pl.ds(r - lo, z.fields, stride=hi - lo), :] = v


def get_row(z, chunk, in_ref, r):
    lo, hi = z.chunks[chunk]
    return in_ref[pl.ds(r - lo, z.fields, stride=hi - lo), :]


def clip(z, cut):
    return min(cut + 2, z.blocks), min(cut + 1, z.blocks), cut


def open_kernel(z, x_hbm, step_ref, off_ref, owner_ref, place0, place1, place2, place3, ls_hbm, h_hbm, emb_hbm, w1_hbm, w2_hbm, w3_hbm,
                inc_ref, x_ref, w1s, w2v, w3s, bias, par, xs, u1, u2,
                ls_ref, h_ref, emb_ref, w1_ref, w3_ref, sems):
    copies = [pltpu.make_async_copy(src, dst, sems.at[k]) for k, (src, dst) in enumerate([
        (ls_hbm, ls_ref), (h_hbm, h_ref), (emb_hbm, emb_ref), (x_hbm, x_ref), (w1_hbm, w1_ref),
        (w2_hbm, w2v), (w3_hbm, w3_ref)])]
    for copy in copies:
        copy.start()
    body = Body(z, w1s, w2v, w3s, bias, par, xs, u1, u2)
    body.clear_edges()
    for copy in copies[:3]:
        copy.wait()
    total = step_ref[0] + off_ref[0]
    row = jnp.where(total >= z.table, total - z.table, total)
    log_noise = ls_ref[row]
    par[0:1, :] = jnp.full((1, z.cols), h_ref[row], F32)
    par[1:2, :] = jnp.where(owner_ref[0] == 0, jnp.ones((1, z.cols), F32), jnp.zeros((1, z.cols), F32))
    par[2:3, :] = jnp.where(owner_ref[0] % 2 == 1, jnp.ones((1, z.cols), F32), jnp.zeros((1, z.cols), F32))
    for t in range(z.hidden // z.cols):
        e = emb_ref[t:t + 1, :] * log_noise
        bias[t * z.cols:(t + 1) * z.cols, :] = jnp.broadcast_to(e, (z.cols, z.cols)).T
    copies[3].wait()
    for r in range(z.rows):
        body.load_row(r, own_rows(z, x_ref, r))
    copies[4].wait()
    for a in range(3):
        parts = [w1_ref[3 * a + b].astype(F32) for b in range(3)]
        if z.kin > 3 * z.fields:
            parts.append(jnp.zeros((z.kin - 3 * z.fields, z.hidden), F32))
        w1s[a] = jnp.concatenate(parts, axis=0).astype(BF16)

    def before3():
        copies[6].wait()
        for a in range(3):
            for b in range(3):
                w3s[a, b * z.mout:b * z.mout + z.fields, :] = w3_ref[3 * a + b]
                if z.mout > z.fields:
                    w3s[a, b * z.mout + z.fields:(b + 1) * z.mout, :] = jnp.zeros((z.mout - z.fields, z.hidden), BF16)

    is_first = par[1:2, :] > 0.0

    def emit(r, v):
        put_row(z, 0, inc_ref, r, v + jnp.where(is_first, own_rows(z, x_ref, r), 0.0))

    body.run((0, 0, 0), clip(z, z.cut), emit, copies[5].wait, before3)


def close_kernel(z, x_ref, w1s, w2, w3s, bias, par, xs_in, u1_in, u2_in, inc_ref, xs, u1, u2):
    body = Body(z, w1s, w2, w3s, bias, par, xs, u1, u2)
    is_first = par[1:2, :] > 0.0

    def emit(r, v):
        put_row(z, 1, inc_ref, r, v + jnp.where(is_first, own_rows(z, x_ref, r), 0.0))

    body.run(clip(z, z.cut), (z.blocks,) * 3, emit)


def early(z):
    return max(z.cut - 1, 0), max(z.cut - 2, 0), 0


def assemble(f_ref, part, rest, mate, par, inc=None):
    length, half = f_ref.shape[0], part.shape[0]
    cut = length - half
    odd = par[2:3, :] > 0.0
    extra = jnp.where(odd, mate[...], 0.0)
    if inc is not None:
        extra = extra + inc[...]
    a, b = part[...], rest[...]
    f_ref[:cut, :] = jnp.where(odd, b[:cut], a[:cut]) + extra[:cut]
    f_ref[cut:, :] = jnp.where(odd, a, b) + extra[cut:]


def early_kernel(z, x_ref, part, rest, mate, w1s, w2_hbm, bias, par, w2, xs, u1, u2, f_ref, sem):
    copy = pltpu.make_async_copy(w2_hbm, w2, sem)
    copy.start()
    body = Body(z, w1s, w2, None, bias, par, xs, u1, u2)
    body.clear_edges()
    assemble(f_ref, part, rest, mate, par)
    is_first = par[1:2, :] > 0.0
    for r in range(*z.chunks[0]):
        body.load_row(r, jnp.where(is_first, own_rows(z, x_ref, r), get_row(z, 0, f_ref, r)))
    ends = early(z)
    body.run((0, 0, 0), (ends[0], 0, 0), None)
    copy.wait()
    body.run((ends[0], 0, 0), ends, None)


def later_kernel(z, x_ref, part, rest, mate, w1s, w2, w3s, bias, par, xs_in, u1_in, u2_in, inc_ref, xs, u1, u2, f_ref):
    body = Body(z, w1s, w2, w3s, bias, par, xs, u1, u2)
    assemble(f_ref, part, rest, mate, par)
    is_first = par[1:2, :] > 0.0
    for r in range(*z.chunks[1]):
        body.load_row(r, jnp.where(is_first, own_rows(z, x_ref, r), get_row(z, 1, f_ref, r)))

    def emit(r, v):
        put_row(z, 0, inc_ref, r, v + jnp.where(is_first, own_rows(z, x_ref, r), 0.0))

    body.run(early(z), clip(z, z.cut), emit)


def groups(z):
    step = up(-(-z.fields // 4), 8)
    return [(lo, min(step, z.fields - lo)) for lo in range(0, z.fields, step)]


def merge_rows(z, chunk, f_ref, o_ref, first, count):
    lo, hi = z.chunks[chunk]
    for r in range(lo, hi):
        o_ref[pl.ds(first * z.rows + r, count, stride=z.rows), :] = f_ref[pl.ds(first * (hi - lo) + r - lo, count, stride=hi - lo), :]


def merge0_kernel(z, part, rest, mate, inc, par, o_ref, f_ref):
    assemble(f_ref, part, rest, mate, par, inc)
    merge_rows(z, 0, f_ref, o_ref, 0, z.fields)


def merge1_kernel(z, part, rest, mate, inc, par, o_in, o_hbm, o_ref, f_ref, sems):
    assemble(f_ref, part, rest, mate, par, inc)
    copies = []
    for k, (first, count) in enumerate(groups(z)):
        merge_rows(z, 1, f_ref, o_ref, first, count)
        place = pl.ds(first * z.rows, count * z.rows)
        copies.append(pltpu.make_async_copy(o_ref.at[place, :], o_hbm.at[place, :], sems.at[k]))
        copies[-1].start()
    for copy in copies:
        copy.wait()


VMEM = pl.BlockSpec(memory_space=pltpu.VMEM)
SMEM = pl.BlockSpec(memory_space=pltpu.SMEM)
HBM = pl.BlockSpec(memory_space=pltpu.HBM)


def shape(*dims, dtype=F32):
    return jax.ShapeDtypeStruct(dims, dtype)


def params():
    return pltpu.CompilerParams(vmem_limit_bytes=20 << 20)


def cost(z, share):
    flops = int(share * 2 * z.rows * z.cols * 9 * z.hidden * (2 * z.fields + z.hidden))
    return pl.CostEstimate(flops=flops, transcendentals=int(share * 2 * z.hidden * z.rows * z.cols), bytes_accessed=1 << 20)


class Program:
    def __init__(self, z):
        self.z = z
        self.state = [shape(z.kin, z.long, dtype=BF16), shape(3, z.hidden, z.long, dtype=BF16), shape(z.hidden, z.long, dtype=BF16)]

    def chunk_shape(self, chunk):
        lo, hi = self.z.chunks[chunk]
        return shape(self.z.fields * (hi - lo), self.z.cols)

    def open(self, x, slab_steps, offset, owner, places, log_sigma, step_size, embed, w1t, w2, w3):
        z = self.z
        outs = [self.chunk_shape(0), shape(*x.shape), shape(3, z.kin, z.hidden, dtype=BF16), shape(*w2.shape, dtype=BF16),
                shape(3, 3 * z.mout, z.hidden, dtype=BF16), shape(z.hidden, z.cols), shape(8, z.cols)] + self.state
        far = [pltpu.with_memory_space_constraint(v, pltpu.HBM) for v in (log_sigma, step_size, embed, w1t, w2, w3)]
        res = pl.pallas_call(
            lambda *refs: open_kernel(z, *refs), out_shape=outs,
            in_specs=[HBM, SMEM, SMEM, SMEM] + [SMEM] * 4 + [HBM] * 6, out_specs=[VMEM] * len(outs),
            scratch_shapes=[pltpu.SMEM((z.table,), F32), pltpu.SMEM((z.table,), F32), pltpu.VMEM(embed.shape, F32),
                            pltpu.VMEM(w1t.shape, BF16), pltpu.VMEM(w3.shape, BF16), pltpu.SemaphoreType.DMA((7,))],
            compiler_params=params(), cost_estimate=cost(z, 0.7), name="open",
        )(pltpu.with_memory_space_constraint(x, pltpu.HBM), slab_steps, offset, owner, *[v.reshape(1) for v in places], *far)
        self.w2 = res[3]
        self.fixed = list(res[2:7])
        self.x = res[1]
        return res[0], list(res[7:])

    def close(self, state):
        z = self.z
        ins = [self.x, *self.fixed, *state]
        outs = [self.chunk_shape(1)] + self.state
        res = pl.pallas_call(
            lambda *refs: close_kernel(z, *refs), out_shape=outs, in_specs=[VMEM] * len(ins), out_specs=[VMEM] * len(outs),
            input_output_aliases={len(ins) - 3 + k: 1 + k for k in range(3)},
            compiler_params=params(), cost_estimate=cost(z, 0.3), name="close",
        )(*ins)
        return res[0]

    def early(self, x, w2, scan):
        z = self.z
        self.x = x
        w1s, _, _, bias, par = self.fixed
        ins = [x, *scan, w1s, pltpu.with_memory_space_constraint(w2, pltpu.HBM), bias, par]
        outs = [shape(*w2.shape, dtype=BF16)] + self.state
        res = pl.pallas_call(
            lambda *refs: early_kernel(z, *refs), out_shape=outs, in_specs=[VMEM] * 5 + [HBM] + [VMEM] * 2,
            out_specs=[VMEM] * len(outs),
            scratch_shapes=[pltpu.VMEM(self.chunk_shape(0).shape, F32), pltpu.SemaphoreType.DMA],
            compiler_params=params(), cost_estimate=cost(z, 0.2), name="early",
        )(*ins)
        self.fixed[1] = res[0]
        return list(res[1:])

    def later(self, scan, state):
        z = self.z
        ins = [self.x, *scan, *self.fixed, *state]
        outs = [self.chunk_shape(0)] + self.state
        res = pl.pallas_call(
            lambda *refs: later_kernel(z, *refs), out_shape=outs, in_specs=[VMEM] * len(ins), out_specs=[VMEM] * len(outs),
            input_output_aliases={len(ins) - 3 + k: 1 + k for k in range(3)},
            scratch_shapes=[pltpu.VMEM(self.chunk_shape(1).shape, F32)],
            compiler_params=params(), cost_estimate=cost(z, 0.5), name="later",
        )(*ins)
        return res[0], list(res[1:])

    def merge0(self, scan, inc):
        z = self.z
        return pl.pallas_call(
            lambda *refs: merge0_kernel(z, *refs), out_shape=shape(z.fields * z.rows, z.cols),
            in_specs=[VMEM] * 5, out_specs=VMEM, scratch_shapes=[pltpu.VMEM(self.chunk_shape(0).shape, F32)],
            compiler_params=params(), name="merge0",
        )(*scan, inc, self.fixed[4])

    def merge1(self, scan, inc, out):
        z = self.z
        return pl.pallas_call(
            lambda *refs: merge1_kernel(z, *refs), out_shape=[shape(*out.shape), shape(*out.shape)],
            in_specs=[VMEM] * 6, out_specs=[HBM, VMEM], input_output_aliases={5: 1},
            scratch_shapes=[pltpu.VMEM(self.chunk_shape(1).shape, F32), pltpu.SemaphoreType.DMA((len(groups(z)),))],
            compiler_params=params(), name="merge1",
        )(*scan, inc, self.fixed[4], out)[0]


def swap(value, step):
    return lax.ppermute(value, "tm", [(j, j ^ step) for j in range(lax.axis_size("tm"))])


def places_of(owner, length):
    half = up(length // 2, 8)
    quarter = up(half // 2, 8)
    base = (owner & 1) * (length - half)
    side = (owner >> 1) & 1
    return base + side * (half - quarter), base + (1 - side) * (half - quarter)


def earlier_sum(increment, owner, places):
    owners = lax.axis_size("tm")
    length = increment.shape[0]
    half = up(length // 2, 8)
    quarter = up(half // 2, 8)
    side = (owner >> 1) & 1
    mate = swap(increment, 1)
    pair = increment + mate
    own = lax.dynamic_slice(pair, (places[0], 0), (quarter, pair.shape[1]), allow_negative_indices=False)
    theirs = lax.dynamic_slice(pair, (places[1], 0), (quarter, pair.shape[1]), allow_negative_indices=False)
    got = swap(theirs, 2)
    near = swap(own, 4)
    cross = swap(theirs, 6)
    below = near + cross
    total = own + got + below
    before = jnp.where((owner & 4) != 0, below, 0.0)
    for k in range(3, owners.bit_length() - 1):
        far = swap(total, 1 << k)
        before = before + jnp.where((owner & (1 << k)) != 0, far, 0.0)
        total = total + far
    back = swap(before + jnp.where(side == 0, own, 0.0), 2)
    here = before + jnp.where(side == 1, got, 0.0)
    low = jnp.where(side == 0, here, back)
    high = jnp.where(side == 0, back, here)
    part = jnp.concatenate([low[: half - quarter], high], axis=0)
    rest = swap(part, 1)
    return part, rest, mate


def shards(states, slab_steps, offset, log_sigma, step_size, w_in, w_mid, w_out, embed):
    owner = lax.axis_index("tm")
    _, fields, rows, cols = states.shape
    z = Sizes(fields, w_in.shape[1], rows, cols, log_sigma.shape[0])
    program = Program(z)
    where = owner.reshape(1).astype(jnp.int32)
    x = states.reshape(fields * rows, cols)
    places = [places_of(owner, fields * (hi - lo)) for lo, hi in z.chunks]
    for sweep_index in range(SWEEPS):
        if sweep_index == 0:
            inc0, state = program.open(x, slab_steps, offset, where, (*places[0], *places[1]), log_sigma, step_size, embed.reshape(-1, cols),
                                       w_in.transpose(0, 2, 1), w_mid, w_out)
        else:
            state = program.early(x, w_mid, scan0)
            inc0, state = program.later(scan1, state)
        inc1 = program.close(state)
        scan0 = earlier_sum(inc0, owner, places[0])
        scan1 = earlier_sum(inc1, owner, places[1])
    out = program.merge0(scan0, inc0)
    return program.merge1(scan1, inc1, out).reshape(states.shape)


def solution(mesh):
    in_specs = (
        P(("grp", "tm"), None, None, None),
        P(("grp", "tm")),
        P("grp"),
        P(),
        P(),
        P(),
        P(),
        P(),
        P(),
    )
    out_specs = P(("grp", "tm"), None, None, None)
    return jax.shard_map(shards, mesh=mesh, in_specs=in_specs, out_specs=out_specs, check_vma=False)
```

```python
import jax
import jax.numpy as jnp
from jax import lax
from jax.experimental import pallas as pl
from jax.experimental.pallas import tpu as pltpu
from jax.sharding import PartitionSpec as P


SWEEPS = 2
BF16 = jnp.bfloat16
F32 = jnp.float32


def up(v, m):
    return -(-v // m) * m


class Sizes:
    def __init__(self, fields, hidden, rows, cols, table):
        self.fields, self.hidden, self.rows, self.cols, self.table = fields, hidden, rows, cols, table
        self.per = 2 if rows % 2 == 0 else 1
        self.blocks = rows // self.per
        self.wide = self.per * cols
        self.kin = up(3 * fields, 16)
        self.mout = up(fields, 16)
        self.cut = (self.blocks + 1) // 2
        self.chunks = ((0, self.cut * self.per), (self.cut * self.per, rows))
        self.long = (rows + 2) * cols


class Body:
    def __init__(self, z, w1s, w2, w3s, bias, par, xs, u1, u2):
        self.z, self.w1s, self.w2, self.w3s, self.bias, self.par = z, w1s, w2, w3s, bias, par
        self.xs, self.u1, self.u2 = xs, u1, u2
        lane = lax.broadcasted_iota(jnp.int32, (1, z.cols), 1)
        self.first_col = lane == 0
        self.last_col = lane == z.cols - 1

    def right(self, v):
        return jnp.where(self.first_col, 0.0, pltpu.roll(v, 1, 1))

    def left(self, v):
        return jnp.where(self.last_col, 0.0, pltpu.roll(v, self.z.cols - 1, 1))

    def clear_edges(self):
        z = self.z
        zx = jnp.zeros((z.kin, z.cols), BF16)
        zu = jnp.zeros((z.hidden, z.cols), BF16)
        for edge in (0, (z.rows + 1) * z.cols):
            self.xs[:, edge:edge + z.cols] = zx
            self.u2[:, edge:edge + z.cols] = zu
            for b in range(3):
                self.u1[b, :, edge:edge + z.cols] = zu

    def load_row(self, r, v):
        z = self.z
        parts = [self.right(v), v, self.left(v)]
        if z.kin > 3 * z.fields:
            parts.append(jnp.zeros((z.kin - 3 * z.fields, z.cols), F32))
        self.xs[:, (r + 1) * z.cols:(r + 2) * z.cols] = jnp.concatenate(parts, axis=0).astype(BF16)

    def silu(self, t):
        return t / (1.0 + jnp.exp(-t))

    def conv1(self, n):
        z = self.z
        acc = None
        for a in range(3):
            lo = (n * z.per + a) * z.cols
            d = lax.dot_general(self.w1s[a], self.xs[:, lo:lo + z.wide], (((0,), (0,)), ((), ())),
                                preferred_element_type=F32)
            acc = d if acc is None else acc + d
        for i in range(z.per):
            lo = (n * z.per + i + 1) * z.cols
            v = self.silu(acc[:, i * z.cols:(i + 1) * z.cols] + self.bias[...])
            self.u1[0, :, lo:lo + z.cols] = self.right(v).astype(BF16)
            self.u1[1, :, lo:lo + z.cols] = v.astype(BF16)
            self.u1[2, :, lo:lo + z.cols] = self.left(v).astype(BF16)

    def conv2(self, n):
        z = self.z
        acc = None
        for a in range(3):
            lo = (n * z.per + a) * z.cols
            for b in range(3):
                d = jnp.dot(self.w2[3 * a + b], self.u1[b, :, lo:lo + z.wide], preferred_element_type=F32)
                acc = d if acc is None else acc + d
        lo = (n * z.per + 1) * z.cols
        self.u2[:, lo:lo + z.wide] = self.silu(acc).astype(BF16)

    def conv3(self, n, emit):
        z = self.z
        acc = None
        for a in range(3):
            lo = (n * z.per + a) * z.cols
            d = jnp.dot(self.w3s[a], self.u2[:, lo:lo + z.wide], preferred_element_type=F32)
            acc = d if acc is None else acc + d
        for i in range(z.per):
            y = acc[:, i * z.cols:(i + 1) * z.cols]
            out = self.right(y[:z.fields]) + y[z.mout:z.mout + z.fields] + self.left(y[2 * z.mout:2 * z.mout + z.fields])
            emit(n * z.per + i, out * self.par[0:1, :])

    def run(self, begin, end, emit, before2=None, before3=None):
        for n in range(self.z.blocks + 2):
            if begin[0] <= n < end[0]:
                self.conv1(n)
            if begin[1] <= n - 1 < end[1]:
                if before2 is not None:
                    before2()
                    before2 = None
                self.conv2(n - 1)
            if begin[2] <= n - 2 < end[2]:
                if before3 is not None:
                    before3()
                    before3 = None
                self.conv3(n - 2, emit)


def own_rows(z, x_ref, r):
    return x_ref[pl.ds(r, z.fields, stride=z.rows), :]


def put_row(z, chunk, out_ref, r, v):
    lo, hi = z.chunks[chunk]
    out_ref[pl.ds(r - lo, z.fields, stride=hi - lo), :] = v


def get_row(z, chunk, in_ref, r):
    lo, hi = z.chunks[chunk]
    return in_ref[pl.ds(r - lo, z.fields, stride=hi - lo), :]


def clip(z, cut):
    return z.blocks, min(cut + 1, z.blocks), cut


def open_kernel(z, x_hbm, step_ref, off_ref, owner_ref, place0, place1, place2, place3, ls_hbm, h_hbm, emb_hbm, w1_hbm, w2_hbm, w3_hbm,
                inc_ref, x_ref, w1s, w2v, w3s, bias, par, xs, u1, u2,
                ls_ref, h_ref, emb_ref, w1_ref, w3_ref, sems):
    copies = [pltpu.make_async_copy(src, dst, sems.at[k]) for k, (src, dst) in enumerate([
        (ls_hbm, ls_ref), (h_hbm, h_ref), (emb_hbm, emb_ref), (x_hbm, x_ref), (w1_hbm, w1_ref),
        (w2_hbm, w2v), (w3_hbm, w3_ref)])]
    for copy in copies:
        copy.start()
    body = Body(z, w1s, w2v, w3s, bias, par, xs, u1, u2)
    body.clear_edges()
    for copy in copies[:3]:
        copy.wait()
    total = step_ref[0] + off_ref[0]
    row = jnp.where(total >= z.table, total - z.table, total)
    log_noise = ls_ref[row]
    par[0:1, :] = jnp.full((1, z.cols), h_ref[row], F32)
    par[1:2, :] = jnp.where(owner_ref[0] == 0, jnp.ones((1, z.cols), F32), jnp.zeros((1, z.cols), F32))
    par[2:3, :] = jnp.where(owner_ref[0] % 2 == 1, jnp.ones((1, z.cols), F32), jnp.zeros((1, z.cols), F32))
    for t in range(z.hidden // z.cols):
        e = emb_ref[t:t + 1, :] * log_noise
        bias[t * z.cols:(t + 1) * z.cols, :] = jnp.broadcast_to(e, (z.cols, z.cols)).T
    copies[3].wait()
    for r in range(z.rows):
        body.load_row(r, own_rows(z, x_ref, r))
    copies[4].wait()
    for a in range(3):
        parts = [w1_ref[3 * a + b].astype(F32) for b in range(3)]
        if z.kin > 3 * z.fields:
            parts.append(jnp.zeros((z.kin - 3 * z.fields, z.hidden), F32))
        w1s[a] = jnp.concatenate(parts, axis=0).astype(BF16)

    def before3():
        copies[6].wait()
        for a in range(3):
            for b in range(3):
                w3s[a, b * z.mout:b * z.mout + z.fields, :] = w3_ref[3 * a + b]
                if z.mout > z.fields:
                    w3s[a, b * z.mout + z.fields:(b + 1) * z.mout, :] = jnp.zeros((z.mout - z.fields, z.hidden), BF16)

    is_first = par[1:2, :] > 0.0

    def emit(r, v):
        put_row(z, 0, inc_ref, r, v + jnp.where(is_first, own_rows(z, x_ref, r), 0.0))

    body.run((0, 0, 0), clip(z, z.cut), emit, copies[5].wait, before3)


def close_kernel(z, x_ref, w1s, w2, w3s, bias, par, xs_in, u1_in, u2_in, inc_ref, xs, u1, u2):
    body = Body(z, w1s, w2, w3s, bias, par, xs, u1, u2)
    is_first = par[1:2, :] > 0.0

    def emit(r, v):
        put_row(z, 1, inc_ref, r, v + jnp.where(is_first, own_rows(z, x_ref, r), 0.0))

    body.run(clip(z, z.cut), (z.blocks,) * 3, emit)


def early(z):
    return max(z.cut - 1, 0), max(z.cut - 2, 0), 0


def assemble(f_ref, part, rest, mate, par, inc=None):
    length, half = f_ref.shape[0], part.shape[0]
    cut = length - half
    odd = par[2:3, :] > 0.0
    extra = jnp.where(odd, mate[...], 0.0)
    if inc is not None:
        extra = extra + inc[...]
    a, b = part[...], rest[...]
    f_ref[:cut, :] = jnp.where(odd, b[:cut], a[:cut]) + extra[:cut]
    f_ref[cut:, :] = jnp.where(odd, a, b) + extra[cut:]


def fetch_kernel(src, dst, sem):
    copy = pltpu.make_async_copy(src, dst, sem)
    copy.start()
    copy.wait()


def early_kernel(z, x_ref, part, rest, mate, w1s, w2, bias, par, xs, u1, u2, f_ref):
    body = Body(z, w1s, w2, None, bias, par, xs, u1, u2)
    body.clear_edges()
    assemble(f_ref, part, rest, mate, par)
    is_first = par[1:2, :] > 0.0
    for r in range(*z.chunks[0]):
        body.load_row(r, jnp.where(is_first, own_rows(z, x_ref, r), get_row(z, 0, f_ref, r)))
    ends = early(z)
    body.run((0, 0, 0), ends, None)


def later_kernel(z, x_ref, part, rest, mate, w1s, w2, w3s, bias, par, xs_in, u1_in, u2_in, inc_ref, xs, u1, u2, f_ref):
    body = Body(z, w1s, w2, w3s, bias, par, xs, u1, u2)
    assemble(f_ref, part, rest, mate, par)
    is_first = par[1:2, :] > 0.0
    for r in range(*z.chunks[1]):
        body.load_row(r, jnp.where(is_first, own_rows(z, x_ref, r), get_row(z, 1, f_ref, r)))

    def emit(r, v):
        put_row(z, 0, inc_ref, r, v + jnp.where(is_first, own_rows(z, x_ref, r), 0.0))

    body.run(early(z), clip(z, z.cut), emit)


def groups(z):
    step = up(-(-z.fields // 4), 8)
    return [(lo, min(step, z.fields - lo)) for lo in range(0, z.fields, step)]


def merge_rows(z, chunk, f_ref, o_ref, first, count):
    lo, hi = z.chunks[chunk]
    for r in range(lo, hi):
        o_ref[pl.ds(first * z.rows + r, count, stride=z.rows), :] = f_ref[pl.ds(first * (hi - lo) + r - lo, count, stride=hi - lo), :]


def merge0_kernel(z, part, rest, mate, inc, par, o_ref, f_ref):
    assemble(f_ref, part, rest, mate, par, inc)
    merge_rows(z, 0, f_ref, o_ref, 0, z.fields)


def merge1_kernel(z, part, rest, mate, inc, par, o_in, o_hbm, o_ref, f_ref, sems):
    assemble(f_ref, part, rest, mate, par, inc)
    copies = []
    for k, (first, count) in enumerate(groups(z)):
        merge_rows(z, 1, f_ref, o_ref, first, count)
        place = pl.ds(first * z.rows, count * z.rows)
        copies.append(pltpu.make_async_copy(o_ref.at[place, :], o_hbm.at[place, :], sems.at[k]))
        copies[-1].start()
    for copy in copies:
        copy.wait()


VMEM = pl.BlockSpec(memory_space=pltpu.VMEM)
SMEM = pl.BlockSpec(memory_space=pltpu.SMEM)
HBM = pl.BlockSpec(memory_space=pltpu.HBM)


def shape(*dims, dtype=F32):
    return jax.ShapeDtypeStruct(dims, dtype)


def params():
    return pltpu.CompilerParams(vmem_limit_bytes=20 << 20)


def cost(z, share):
    flops = int(share * 2 * z.rows * z.cols * 9 * z.hidden * (2 * z.fields + z.hidden))
    return pl.CostEstimate(flops=flops, transcendentals=int(share * 2 * z.hidden * z.rows * z.cols), bytes_accessed=1 << 20)


class Program:
    def __init__(self, z):
        self.z = z
        self.state = [shape(z.kin, z.long, dtype=BF16), shape(3, z.hidden, z.long, dtype=BF16), shape(z.hidden, z.long, dtype=BF16)]

    def chunk_shape(self, chunk):
        lo, hi = self.z.chunks[chunk]
        return shape(self.z.fields * (hi - lo), self.z.cols)

    def open(self, x, slab_steps, offset, owner, places, log_sigma, step_size, embed, w1t, w2, w3):
        z = self.z
        outs = [self.chunk_shape(0), shape(*x.shape), shape(3, z.kin, z.hidden, dtype=BF16), shape(*w2.shape, dtype=BF16),
                shape(3, 3 * z.mout, z.hidden, dtype=BF16), shape(z.hidden, z.cols), shape(8, z.cols)] + self.state
        far = [pltpu.with_memory_space_constraint(v, pltpu.HBM) for v in (log_sigma, step_size, embed, w1t, w2, w3)]
        res = pl.pallas_call(
            lambda *refs: open_kernel(z, *refs), out_shape=outs,
            in_specs=[HBM, SMEM, SMEM, SMEM] + [SMEM] * 4 + [HBM] * 6, out_specs=[VMEM] * len(outs),
            scratch_shapes=[pltpu.SMEM((z.table,), F32), pltpu.SMEM((z.table,), F32), pltpu.VMEM(embed.shape, F32),
                            pltpu.VMEM(w1t.shape, BF16), pltpu.VMEM(w3.shape, BF16), pltpu.SemaphoreType.DMA((7,))],
            compiler_params=params(), cost_estimate=cost(z, 0.7), name="open",
        )(pltpu.with_memory_space_constraint(x, pltpu.HBM), slab_steps, offset, owner, *[v.reshape(1) for v in places], *far)
        self.w2 = res[3]
        self.fixed = list(res[2:7])
        self.x = res[1]
        return res[0], list(res[7:])

    def close(self, state):
        z = self.z
        ins = [self.x, *self.fixed, *state]
        outs = [self.chunk_shape(1)] + self.state
        res = pl.pallas_call(
            lambda *refs: close_kernel(z, *refs), out_shape=outs, in_specs=[VMEM] * len(ins), out_specs=[VMEM] * len(outs),
            input_output_aliases={len(ins) - 3 + k: 1 + k for k in range(3)},
            compiler_params=params(), cost_estimate=cost(z, 0.3), name="close",
        )(*ins)
        return res[0]

    def early(self, x, w2, scan):
        z = self.z
        self.x = x
        w1s, _, _, bias, par = self.fixed
        self.fixed[1] = w2
        ins = [x, *scan, w1s, w2, bias, par]
        outs = self.state
        res = pl.pallas_call(
            lambda *refs: early_kernel(z, *refs), out_shape=outs, in_specs=[VMEM] * len(ins), out_specs=[VMEM] * len(outs),
            scratch_shapes=[pltpu.VMEM(self.chunk_shape(0).shape, F32)],
            compiler_params=params(), cost_estimate=cost(z, 0.2), name="early",
        )(*ins)
        return list(res)

    def fetch(self, w2):
        return pl.pallas_call(
            fetch_kernel, out_shape=shape(*w2.shape, dtype=BF16), in_specs=[HBM], out_specs=VMEM,
            scratch_shapes=[pltpu.SemaphoreType.DMA], compiler_params=pltpu.CompilerParams(vmem_limit_bytes=1 << 20), name="fetch",
        )(pltpu.with_memory_space_constraint(w2, pltpu.HBM))

    def later(self, scan, state):
        z = self.z
        ins = [self.x, *scan, *self.fixed, *state]
        outs = [self.chunk_shape(0)] + self.state
        res = pl.pallas_call(
            lambda *refs: later_kernel(z, *refs), out_shape=outs, in_specs=[VMEM] * len(ins), out_specs=[VMEM] * len(outs),
            input_output_aliases={len(ins) - 3 + k: 1 + k for k in range(3)},
            scratch_shapes=[pltpu.VMEM(self.chunk_shape(1).shape, F32)],
            compiler_params=params(), cost_estimate=cost(z, 0.5), name="later",
        )(*ins)
        return res[0], list(res[1:])

    def merge0(self, scan, inc):
        z = self.z
        return pl.pallas_call(
            lambda *refs: merge0_kernel(z, *refs), out_shape=shape(z.fields * z.rows, z.cols),
            in_specs=[VMEM] * 5, out_specs=VMEM, scratch_shapes=[pltpu.VMEM(self.chunk_shape(0).shape, F32)],
            compiler_params=params(), name="merge0",
        )(*scan, inc, self.fixed[4])

    def merge1(self, scan, inc, out):
        z = self.z
        return pl.pallas_call(
            lambda *refs: merge1_kernel(z, *refs), out_shape=[shape(*out.shape), shape(*out.shape)],
            in_specs=[VMEM] * 6, out_specs=[HBM, VMEM], input_output_aliases={5: 1},
            scratch_shapes=[pltpu.VMEM(self.chunk_shape(1).shape, F32), pltpu.SemaphoreType.DMA((len(groups(z)),))],
            compiler_params=params(), name="merge1",
        )(*scan, inc, self.fixed[4], out)[0]


def swap(value, step):
    return lax.ppermute(value, "tm", [(j, j ^ step) for j in range(lax.axis_size("tm"))])


def places_of(owner, length):
    half = up(length // 2, 8)
    quarter = up(half // 2, 8)
    base = (owner & 1) * (length - half)
    side = (owner >> 1) & 1
    return base + side * (half - quarter), base + (1 - side) * (half - quarter)


def earlier_sum(increment, owner, places):
    owners = lax.axis_size("tm")
    length = increment.shape[0]
    half = up(length // 2, 8)
    quarter = up(half // 2, 8)
    side = (owner >> 1) & 1
    mate = swap(increment, 1)
    pair = increment + mate
    own = lax.dynamic_slice(pair, (places[0], 0), (quarter, pair.shape[1]), allow_negative_indices=False)
    theirs = lax.dynamic_slice(pair, (places[1], 0), (quarter, pair.shape[1]), allow_negative_indices=False)
    got = swap(theirs, 2)
    near = swap(own, 4)
    cross = swap(theirs, 6)
    below = near + cross
    total = own + got + below
    before = jnp.where((owner & 4) != 0, below, 0.0)
    for k in range(3, owners.bit_length() - 1):
        far = swap(total, 1 << k)
        before = before + jnp.where((owner & (1 << k)) != 0, far, 0.0)
        total = total + far
    back = swap(before + jnp.where(side == 0, own, 0.0), 2)
    here = before + jnp.where(side == 1, got, 0.0)
    low = jnp.where(side == 0, here, back)
    high = jnp.where(side == 0, back, here)
    part = jnp.concatenate([low[: half - quarter], high], axis=0)
    rest = swap(part, 1)
    return part, rest, mate


def shards(states, slab_steps, offset, log_sigma, step_size, w_in, w_mid, w_out, embed):
    owner = lax.axis_index("tm")
    _, fields, rows, cols = states.shape
    z = Sizes(fields, w_in.shape[1], rows, cols, log_sigma.shape[0])
    program = Program(z)
    where = owner.reshape(1).astype(jnp.int32)
    x = states.reshape(fields * rows, cols)
    places = [places_of(owner, fields * (hi - lo)) for lo, hi in z.chunks]
    for sweep_index in range(SWEEPS):
        if sweep_index == 0:
            inc0, state = program.open(x, slab_steps, offset, where, (*places[0], *places[1]), log_sigma, step_size, embed.reshape(-1, cols),
                                       w_in.transpose(0, 2, 1), w_mid, w_out)
        else:
            near2 = program.fetch(w_mid)
            state = program.early(x, near2, scan0)
            inc0, state = program.later(scan1, state)
        inc1 = program.close(state)
        scan0 = earlier_sum(inc0, owner, places[0])
        scan1 = earlier_sum(inc1, owner, places[1])
    out = program.merge0(scan0, inc0)
    return program.merge1(scan1, inc1, out).reshape(states.shape)


def solution(mesh):
    in_specs = (
        P(("grp", "tm"), None, None, None),
        P(("grp", "tm")),
        P("grp"),
        P(),
        P(),
        P(),
        P(),
        P(),
        P(),
    )
    out_specs = P(("grp", "tm"), None, None, None)
    return jax.shard_map(shards, mesh=mesh, in_specs=in_specs, out_specs=out_specs, check_vma=False)
```
